128 devices in a mesh: lon: 8 (over x, y_hi), lat: 16 (over y_lo, z, core).
Axes of the slice: x: 4, y: 4 (y_hi: 2, y_lo: 2; y = y_hi * 2 + y_lo), z: 4, core: 2. Of those that a mesh axis runs over, the one named last changes fastest.
Arguments:
- field: float32 [32, 768, 3072], P(None, 'lat', 'lon'), may hold values from -6 to 6
- vertical: float32 [32, 32], replicated, may hold values from -1.5 to 1.5, as said below
- rate: float32 [32, 768], P(None, 'lat'), may hold values from 3.2552085e-05 to 0.5
- lat_kernel: float32 [768, 768], replicated, may hold values from 0 to 1, as said below
Outputs:
- increment: float32 [32, 768, 3072], P(None, 'lat', 'lon')
The draws below stay inside these ranges and needn't reach their ends.
Inputs may be any that keep to these rules, and one draw needn't show every extreme that they name: `vertical`: the identity plus independent terms of magnitude at most 0.5 times 4 / sqrt(32). `lat_kernel`: Non-negative weights.
All inputs are finite; a program needn't handle non-finite values.
Results may differ from the reference program's by a relative error of at most 0.00015.
Values sent between devices are 32-bit elements; how exact they have to be, the bound alone decides.
No kernel may reach another device: no remote copies, remote signals or barrier semaphores. Data moves between devices by JAX's collectives and lax.ppermute only.
A program may use at most 128 MiB of HBM per device.

```python
import math
import jax
import jax.numpy as jnp
from jax import lax

LEV = 32
NLAT = 768
NLON = 3072
PASSES = 2


def draw_vertical(key, part):
    noise = jnp.clip(jax.random.normal(key, (LEV, LEV), jnp.float32), -4.0, 4.0)
    return jnp.eye(LEV, dtype=jnp.float32) + 0.5 * noise / jnp.sqrt(jnp.float32(LEV))


def draw_lat_kernel(key, part):
    width = NLAT / 8.0
    rows = jnp.arange(NLAT, dtype=jnp.float32)[:, None]
    cols = jnp.arange(NLAT, dtype=jnp.float32)[None, :]
    base = jnp.exp(-0.5 * ((rows - cols) / width) ** 2) / (width * 2.5066)
    factors = jnp.exp(jax.random.uniform(key, (NLAT, NLAT), jnp.float32, -0.6931, 0.6931))
    return base * factors + 0.5 * jnp.eye(NLAT, dtype=jnp.float32)


def steps_of(key, dims, shards, least, high):
    factor_of, own = 1.0, jax.random.fold_in(key, 6)
    for dim, shards_of in shards:
        heights = jnp.exp(jax.random.uniform(jax.random.fold_in(own, dim), (shards_of,), jnp.float32, least / len(shards), high / len(shards)))
        factor_of = factor_of * jnp.repeat(heights, dims[dim] // shards_of).reshape([-1 if axis == dim else 1 for axis in range(len(dims))])
    return factor_of


def normal_values(rng, extent, scale, reach, cuts=(), held_as=jnp.bfloat16):
    factor_of = steps_of(rng, extent, cuts, -0.22, 0.18) if cuts else 1.0
    result = jax.random.normal(rng, extent, jnp.float32) * scale * factor_of
    return jnp.minimum(jnp.maximum(result, -reach), reach).astype(held_as)


def setup_inputs(seed: int = 0) -> dict:
    arg_keys = jax.random.split(jax.random.key(seed), 5)
    field = normal_values(arg_keys[0], (LEV, NLAT, NLON), 1.0, 6.0, ((1, 16), (2, 8)), jnp.float32)
    vertical = draw_vertical(jax.random.fold_in(arg_keys[4], 71), 0)
    rate = jnp.clip(jnp.exp(math.log(0.5) - 9.639522 * jax.random.uniform(arg_keys[2], (LEV, NLAT), jnp.float32) ** steps_of(arg_keys[2], (LEV, NLAT), ((1, 16),), -0.2, 0.2)), 3.255208503105678e-05, 0.5)
    lat_kernel = draw_lat_kernel(jax.random.fold_in(arg_keys[4], 71), 0)
    return {"field": field, "vertical": vertical, "rate": rate, "lat_kernel": lat_kernel}


def combine(first, second):
    return (first[0] * second[0], second[0] * first[1] + second[1])


def one_level(items):
    rows, level_rate, kernel = items
    log_decay = jnp.log1p(-level_rate)[:, None]
    decay = jnp.exp(log_decay)
    coefficient = level_rate[:, None]
    positions = jnp.arange(NLON, dtype=jnp.float32)[None, :]
    closing = -jnp.expm1(NLON * log_decay[:, 0])
    decays = jnp.broadcast_to(decay, rows.shape)
    for step in range(PASSES):
        east = step % 2 == 0
        filtered = lax.associative_scan(combine, (decays, coefficient * rows), axis=1, reverse=not east)[1]
        if east:
            edge = filtered[:, -1]
            power = jnp.exp((positions + 1.0) * log_decay)
        else:
            edge = filtered[:, 0]
            power = jnp.exp((NLON - positions) * log_decay)
        rows = filtered + power * (edge / closing)[:, None]
    return jnp.dot(kernel, rows, precision=lax.Precision.HIGHEST)


def reference(field, vertical, rate, lat_kernel):
    mixed = jnp.einsum("km,mjn->kjn", vertical, field, precision=lax.Precision.HIGHEST)
    return lax.map(lambda pair: one_level((pair[0], pair[1], lat_kernel)), (mixed, rate))
```

```python
import functools

import jax
import jax.numpy as jnp
from jax import lax
from jax.experimental import pallas as pl
from jax.experimental.pallas import tpu as pltpu
from jax.sharding import PartitionSpec as P

LANES = 128
SUB = 8


def split(x):
    high = x.astype(jnp.bfloat16)
    return high, (x - high.astype(jnp.float32)).astype(jnp.bfloat16)


def dot(a, b):
    return jnp.dot(a, b, preferred_element_type=jnp.float32)


def dot3(a_high, a_low, b_high, b_low):
    return dot(a_high, b_high) + (dot(a_high, b_low) + dot(a_low, b_high))


def filter_kernel(levels, field_ref, vertical_ref, decay_ref, gain_ref, out_ref, edge_ref, high_ref, low_ref, mixed_ref, decays_ref, gains_ref):
    rows = levels * SUB
    depth = vertical_ref.shape[1] * SUB
    tiles = out_ref.shape[2] // LANES

    @pl.when(pl.program_id(0) == 0)
    def _():
        spread = (lax.broadcasted_iota(jnp.int32, (rows, levels), 0) // SUB == lax.broadcasted_iota(jnp.int32, (rows, levels), 1)).astype(jnp.bfloat16)
        across = (lax.broadcasted_iota(jnp.int32, (depth // SUB, depth), 1) // SUB == lax.broadcasted_iota(jnp.int32, (depth // SUB, depth), 0)).astype(jnp.bfloat16)
        same = lax.broadcasted_iota(jnp.int32, (rows, depth), 0) % SUB == lax.broadcasted_iota(jnp.int32, (rows, depth), 1) % SUB
        for part, ref in zip(split(vertical_ref[...]), (high_ref, low_ref)):
            tall = dot(spread, part).astype(jnp.bfloat16)
            ref[...] = jnp.where(same, dot(tall, across), 0.0).astype(jnp.bfloat16)

    x_high, x_low = split(field_ref[...].reshape(depth, tiles * LANES))
    mixed_ref[...] = dot3(high_ref[...], low_ref[...], x_high, x_low)
    for level in range(levels):
        at = slice(level * SUB, (level + 1) * SUB)
        decays_ref[at, :] = jnp.broadcast_to(decay_ref[:, level : level + 1], (SUB, LANES))
        gains_ref[at, :] = jnp.broadcast_to(gain_ref[:, level : level + 1], (SUB, LANES))

    step = 4
    count = step * SUB
    lane = lax.broadcasted_iota(jnp.int32, (count, LANES), 1)
    lane_f = lane.astype(jnp.float32)
    narrow = lax.broadcasted_iota(jnp.int32, (SUB, LANES), 1)

    def body(index, edges):
        at = pl.ds(pl.multiple_of(index * count, count), count)
        log_decay = decays_ref[at, :]
        gain = gains_ref[at, :]
        value = [mixed_ref[at, c * LANES : (c + 1) * LANES] * gain for c in range(tiles)]
        east, west = list(value), list(value)
        power = jnp.exp(log_decay)
        d = 1
        while d < LANES:
            weight_east = jnp.where(lane >= d, power, 0.0)
            weight_west = jnp.where(lane < LANES - d, power, 0.0)
            east = [v + weight_east * pltpu.roll(v, d, 1) for v in east]
            west = [v + weight_west * pltpu.roll(v, LANES - d, 1) for v in west]
            power = power * power
            d *= 2
        reach_east = jnp.exp(log_decay * (lane_f + 1.0))
        reach_west = jnp.exp(log_decay * (LANES - lane_f))
        for c in range(1, tiles):
            east[c] = east[c] + reach_east * jnp.broadcast_to(east[c - 1][:, LANES - 1 :], (count, LANES))
        for c in range(tiles - 2, -1, -1):
            west[c] = west[c] + reach_west * jnp.broadcast_to(west[c + 1][:, :1], (count, LANES))
        for c in range(tiles):
            total = east[c] + west[c] - value[c]
            out_ref[pl.ds(index * step, step), :, c * LANES : (c + 1) * LANES] = total.reshape(step, SUB, LANES)
        last = jnp.broadcast_to(east[-1][:, LANES - 1 :], (count, LANES))
        first = jnp.broadcast_to(west[0][:, :1], (count, LANES))
        for k in range(step):
            here = slice(k * SUB, (k + 1) * SUB)
            edges = jnp.where(narrow == index * step + k, last[here], edges)
            edges = jnp.where(narrow == levels + index * step + k, first[here], edges)
        return edges

    edge_ref[...] = lax.fori_loop(0, levels // step, body, jnp.zeros((SUB, LANES), jnp.float32))


def filtered_blocks(field, vertical, decay, gain):
    depth, lats, lons = field.shape
    levels = vertical.shape[0]
    return pl.pallas_call(
        functools.partial(filter_kernel, levels),
        grid=(lats // SUB,),
        in_specs=[
            pl.BlockSpec((depth, SUB, lons), lambda g: (0, g, 0)),
            pl.BlockSpec((levels, depth), lambda g: (0, 0)),
            pl.BlockSpec((SUB, levels), lambda g: (g, 0)),
            pl.BlockSpec((SUB, levels), lambda g: (g, 0)),
        ],
        out_specs=[
            pl.BlockSpec((levels, SUB, lons), lambda g: (0, g, 0)),
            pl.BlockSpec((SUB, LANES), lambda g: (g, 0)),
        ],
        out_shape=[
            jax.ShapeDtypeStruct((levels, lats, lons), jnp.float32),
            jax.ShapeDtypeStruct((lats, LANES), jnp.float32),
        ],
        scratch_shapes=[
            pltpu.VMEM((levels * SUB, depth * SUB), jnp.bfloat16),
            pltpu.VMEM((levels * SUB, depth * SUB), jnp.bfloat16),
            pltpu.VMEM((levels * SUB, lons), jnp.float32),
            pltpu.VMEM((levels * SUB, LANES), jnp.float32),
            pltpu.VMEM((levels * SUB, LANES), jnp.float32),
        ],
        cost_estimate=pl.CostEstimate(flops=8 * 10**8, bytes_accessed=4 * 10**6, transcendentals=10**5),
        name="mix_filter",
    )(field, vertical, decay, gain)


def convolve_kernel(level, values_ref, state_ref, kernel_ref, *rest):
    out_ref, high_ref, low_ref = rest[-3:]
    sources, lats, lons = values_ref.shape
    tiles = lons // LANES

    @pl.when(pl.program_id(0) == 0)
    def _():
        lane = lax.broadcasted_iota(jnp.int32, (lats, LANES), 1).astype(jnp.float32)
        states = state_ref[...].reshape(sources * SUB, LANES).T

        for source in range(sources):
            def column(which):
                at = source * SUB + 3 * level + which
                return jnp.broadcast_to(states[:lats, at : at + 1], (lats, LANES))

            log_decay = column(2)
            hop = jnp.exp(log_decay * float(LANES))
            from_west = column(0) * jnp.exp(log_decay * (lane + 1.0))
            from_east = column(1) * jnp.exp(log_decay * (LANES - lane))
            wests, easts = [from_west], [from_east]
            for _ in range(tiles - 1):
                wests.append(wests[-1] * hop)
                easts.append(easts[-1] * hop)
            for c in range(tiles):
                cols = slice(c * LANES, (c + 1) * LANES)
                total = values_ref[source, :, cols] + (wests[c] + easts[tiles - 1 - c])
                high, low = split(total)
                high_ref[source * lats : (source + 1) * lats, cols] = high
                low_ref[source * lats : (source + 1) * lats, cols] = low

    k_high, k_low = split(kernel_ref[...])
    result = dot3(k_high, k_low, high_ref[...], low_ref[...])
    out_ref[...] = result.reshape(out_ref.shape)


def convolved(level, values, states, lat_kernel, buffer=None):
    sources, lats, lons = values.shape
    nlat = sources * lats
    group = 4
    held = [] if buffer is None else [buffer]
    return pl.pallas_call(
        functools.partial(convolve_kernel, level),
        grid=(sources // group,),
        in_specs=[
            pl.BlockSpec((sources, lats, lons), lambda j: (0, 0, 0)),
            pl.BlockSpec((sources, SUB, LANES), lambda j: (0, 0, 0)),
            pl.BlockSpec((group * lats, nlat), lambda j: (j, 0)),
        ]
        + [pl.BlockSpec(memory_space=pl.ANY) for _ in held],
        out_specs=pl.BlockSpec((group, 1, lats, lons), lambda j: (j, level, 0, 0)),
        out_shape=jax.ShapeDtypeStruct((sources, 2, lats, lons), jnp.float32),
        scratch_shapes=[
            pltpu.VMEM((nlat, lons), jnp.bfloat16),
            pltpu.VMEM((nlat, lons), jnp.bfloat16),
        ],
        input_output_aliases={3: 0} if held else {},
        cost_estimate=pl.CostEstimate(flops=14 * 10**8, bytes_accessed=5 * 10**6, transcendentals=2 * 10**5),
        name="convolve",
    )(values, states, lat_kernel, *held)


def on_device(field, vertical, rate, lat_kernel):
    ring, owners = lax.axis_size("lon"), lax.axis_size("lat")
    levels, lats, width = field.shape
    half = levels // 2
    log_decay = jnp.log1p(-rate)
    decay_t, gain_t = log_decay.T, (rate / (2.0 - rate)).T
    blocks, edges = [], []
    for part in range(2):
        block, edge = filtered_blocks(field, vertical[part::2], decay_t[:, part::2], gain_t[:, part::2])
        blocks.append(block)
        edges.append(edge[:, : 2 * half])
    edge = jnp.concatenate(edges, 1)
    block_decay = jnp.exp(width * decay_t)
    closing = -jnp.expm1((ring * width) * decay_t)
    powers = [1.0 / closing]
    for _ in range(ring - 1):
        powers.append(powers[-1] * block_decay)
    from_west = from_east = 0.0
    for hop in range(ring):
        there = edge if hop == 0 else lax.ppermute(edge, "lon", [(i, (i + hop) % ring) for i in range(ring)])
        there = there.reshape(lats, 2, 2, half)
        last = there[:, :, 0].transpose(0, 2, 1).reshape(lats, levels)
        first = there[:, :, 1].transpose(0, 2, 1).reshape(lats, levels)
        from_west = from_west + last * powers[(hop - 1) % ring]
        from_east = from_east + first * powers[ring - 1 - hop]
    states = jnp.stack([from_west, from_east, decay_t], 0)
    states = states.reshape(3, lats, owners, 2).transpose(2, 3, 0, 1).reshape(owners, 6, lats)
    states = jnp.pad(states, ((0, 0), (0, SUB - 6), (0, LANES - lats)))

    def to_owner(v):
        return lax.all_to_all(v, "lat", 0, 0, tiled=True)

    first = to_owner(blocks[0])
    states = to_owner(states)
    second = to_owner(blocks[1])
    out = convolved(0, first, states, lat_kernel)
    out = convolved(1, second, states, lat_kernel, out)
    return to_owner(out).reshape(levels, lats, width)


def solution(mesh):
    return jax.shard_map(
        on_device,
        mesh=mesh,
        in_specs=(P(None, "lat", "lon"), P(), P(None, "lat"), P()),
        out_specs=P(None, "lat", "lon"),
        check_vma=False,
    )
```

```python
import functools

import jax
import jax.numpy as jnp
from jax import lax
from jax.experimental import pallas as pl
from jax.experimental.pallas import tpu as pltpu
from jax.sharding import PartitionSpec as P

LANES = 128
SUB = 8
MID = LANES // 2


def split(x):
    high = x.astype(jnp.bfloat16)
    return high, (x - high.astype(jnp.float32)).astype(jnp.bfloat16)


def dot(a, b):
    return jnp.dot(a, b, preferred_element_type=jnp.float32)


def dot3(a_high, a_low, b_high, b_low):
    return dot(a_high, b_high) + (dot(a_high, b_low) + dot(a_low, b_high))


def iota(shape, dim):
    return lax.broadcasted_iota(jnp.int32, shape, dim)


def log_decays(rate):
    decay = 1.0 - rate
    gap = decay - 1.0
    return jnp.log(decay) * (rate / -gap)


def filter_kernel(part, field_ref, vertical_ref, rate_ref, *rest):
    held = rest[:-9]
    out_ref, edge_ref, high_ref, low_ref, sums_east_ref, sums_west_ref, decay_ref, gain_ref, edges_ref = rest[-9:]
    levels = out_ref.shape[0]
    depth = vertical_ref.shape[1]
    rows = levels * SUB
    tiles = out_ref.shape[1]
    group = pl.program_id(0)

    @pl.when(group == 0)
    def _():
        spread = (iota((rows, depth), 0) // SUB * 2 + part == iota((rows, depth), 1)).astype(jnp.bfloat16)
        across = (iota((depth, depth * SUB), 1) // SUB == iota((depth, depth * SUB), 0)).astype(jnp.bfloat16)
        same = iota((rows, depth * SUB), 0) % SUB == iota((rows, depth * SUB), 1) % SUB
        for piece, ref in zip(split(vertical_ref[...]), (high_ref, low_ref)):
            tall = dot(spread, piece).astype(jnp.bfloat16)
            ref[...] = jnp.where(same, dot(tall, across), 0.0).astype(jnp.bfloat16)
        source, target = iota((2 * LANES, 2 * LANES), 0) % LANES, iota((2 * LANES, 2 * LANES), 1)
        sums_east_ref[...] = ((source <= target) | (target >= LANES)).astype(jnp.bfloat16)
        sums_west_ref[...] = ((source > target) | (target >= LANES)).astype(jnp.bfloat16)
        rate = rate_ref[...]
        lats = rate.shape[1]
        filled = jnp.zeros((LANES - depth, LANES), jnp.float32)

        def turned(v):
            wide = jnp.concatenate([v, jnp.zeros((depth, LANES - lats), jnp.float32)], 1)
            return jnp.concatenate([wide, filled], 0).T

        decay_ref[...] = turned(log_decays(rate))
        gain_ref[...] = turned(rate / (2.0 - rate))
        edges_ref[...] = jnp.zeros_like(edges_ref)

    x_high, x_low = split(field_ref[...].reshape(depth * SUB, tiles * LANES))
    mixed = dot3(high_ref[...], low_ref[...], x_high, x_low)
    here = pl.ds(pl.multiple_of(group * SUB, SUB), SUB)

    def on_rows(ref):
        turned = ref[here, :]
        columns = [jnp.broadcast_to(turned[:, 2 * k + part : 2 * k + part + 1], (SUB, LANES)) for k in range(levels)]
        return jnp.concatenate(columns, 0)

    log_decay, gain = on_rows(decay_ref), on_rows(gain_ref)
    offset = (iota((rows, LANES), 1) - MID).astype(jnp.float32) * log_decay
    falling, rising = jnp.exp(offset), jnp.exp(-offset)
    half = jnp.exp(MID * log_decay)
    rising_in, falling_in = rising * gain, falling * gain

    def summed(v, ref):
        high, low = split(v)
        both = dot(jnp.concatenate([high, low], 1), ref[...])
        return both[:, :LANES], both[:, LANES:]

    east, west, carry_east, carry_west = [None] * tiles, [None] * tiles, [None] * tiles, [None] * tiles
    all_east, all_west = [None] * tiles, [None] * tiles
    for c in range(tiles):
        value = mixed[:, c * LANES : (c + 1) * LANES]
        east[c], all_east[c] = summed(value * rising_in, sums_east_ref)
        west[c], all_west[c] = summed(value * falling_in, sums_west_ref)
    carry = 0.0
    for c in range(tiles):
        carry_east[c] = carry
        carry = half * (half * (all_east[c] + carry))
    last = carry * jnp.exp((-LANES + MID - 1) * log_decay)
    carry = 0.0
    for c in range(tiles - 1, -1, -1):
        carry_west[c] = carry
        carry = half * (all_west[c] + carry)
        first = carry
        carry = half * carry
    for c in range(tiles):
        total = falling * (east[c] + carry_east[c]) + rising * (west[c] + carry_west[c])
        out_ref[:, c, :, :] = total.reshape(levels, SUB, LANES)
    lane = iota((SUB, LANES), 1)
    edges = jnp.zeros((SUB, LANES), jnp.float32)
    for k in range(levels):
        at = slice(k * SUB, (k + 1) * SUB)
        edges = jnp.where(lane == k, last[at], edges)
        edges = jnp.where(lane == levels + k, first[at], edges)
    edges_ref[here, :] = edges

    @pl.when(group == pl.num_programs(0) - 1)
    def _():
        own = edges_ref[...].T[: 2 * levels]
        edge_ref[...] = jnp.concatenate([ref[...] for ref in held] + [own], 0)


def filtered_blocks(part, field, vertical, rate, held=()):
    depth, lats, lons = field.shape
    levels, groups, tiles = depth // 2, lats // SUB, lons // LANES
    edges = 2 * levels * (1 + len(held))
    return pl.pallas_call(
        functools.partial(filter_kernel, part),
        grid=(groups,),
        in_specs=[
            pl.BlockSpec((depth, SUB, lons), lambda g: (0, g, 0)),
            pl.BlockSpec(vertical.shape, lambda g: (0, 0)),
            pl.BlockSpec(rate.shape, lambda g: (0, 0)),
        ]
        + [pl.BlockSpec(v.shape, lambda g: (0, 0)) for v in held],
        out_specs=[
            pl.BlockSpec((levels, tiles, SUB, LANES), lambda g: (0, g, 0, 0)),
            pl.BlockSpec((edges, LANES), lambda g: (0, 0)),
        ],
        out_shape=[
            jax.ShapeDtypeStruct((levels, groups * tiles + part, SUB, LANES), jnp.float32),
            jax.ShapeDtypeStruct((edges, LANES), jnp.float32),
        ],
        scratch_shapes=[
            pltpu.VMEM((levels * SUB, depth * SUB), jnp.bfloat16),
            pltpu.VMEM((levels * SUB, depth * SUB), jnp.bfloat16),
            pltpu.VMEM((2 * LANES, 2 * LANES), jnp.bfloat16),
            pltpu.VMEM((2 * LANES, 2 * LANES), jnp.bfloat16),
            pltpu.VMEM((LANES, LANES), jnp.float32),
            pltpu.VMEM((LANES, LANES), jnp.float32),
            pltpu.VMEM((LANES, LANES), jnp.float32),
        ],
        cost_estimate=pl.CostEstimate(flops=8 * 10**8, bytes_accessed=4 * 10**6, transcendentals=10**5),
        name="mix_filter",
    )(field, vertical, rate, *held)


def states_kernel(width, rate_ref, *rest):
    hops, out_ref = rest[:-2], rest[-1]
    ring = len(hops)
    levels = out_ref.shape[0]
    lats = rate_ref.shape[1]
    for part in range(2):
        rate = rate_ref[pl.ds(part, levels, stride=2), :]
        rate = jnp.concatenate([rate, jnp.full((levels, LANES - lats), 0.5, jnp.float32)], 1)
        log_decay = log_decays(rate)
        scale = 1.0 / (1.0 - jnp.exp((ring * width) * log_decay))
        across = jnp.exp(width * log_decay)
        from_west = from_east = jnp.zeros((levels, LANES), jnp.float32)
        power = scale
        for steps in range(ring):
            at = 2 * part * levels
            from_west = from_west + hops[(steps + 1) % ring][at : at + levels, :] * power
            at += levels
            from_east = from_east + hops[ring - 1 - steps][at : at + levels, :] * power
            power = power * across
        for which, value in enumerate((from_west, from_east, log_decay)):
            out_ref[:, 0, 3 * part + which, :] = value
    out_ref[:, 0, 6:, :] = jnp.zeros((levels, 2, LANES), jnp.float32)


def with_states(width, rate, hops, block):
    levels, tiles = block.shape[:2]
    return pl.pallas_call(
        functools.partial(states_kernel, width),
        grid=(1,),
        in_specs=[pl.BlockSpec(v.shape, lambda i: (0, 0)) for v in (rate, *hops)] + [pl.BlockSpec(memory_space=pl.ANY)],
        out_specs=pl.BlockSpec((levels, 1, SUB, LANES), lambda i: (0, tiles - 1, 0, 0)),
        out_shape=jax.ShapeDtypeStruct(block.shape, block.dtype),
        input_output_aliases={1 + len(hops): 0},
        name="states",
    )(rate, *hops, block)


def convolve_kernel(first_ref, second_ref, kernel_ref, out_ref, high_ref, low_ref):
    sources = first_ref.shape[0]
    lats = out_ref.shape[2]
    tiles = out_ref.shape[3] // LANES
    groups = lats // SUB

    @pl.when(pl.program_id(0) == 0)
    def _():
        lane = iota((lats, LANES), 1).astype(jnp.float32)
        states = second_ref[:, groups * tiles].reshape(sources * SUB, LANES).T
        for source in range(sources):
            for part, ref in enumerate((first_ref, second_ref)):
                def column(which):
                    at = source * SUB + 3 * part + which
                    return jnp.broadcast_to(states[:lats, at : at + 1], (lats, LANES))

                log_decay = column(2)
                hop = jnp.exp(log_decay * float(LANES))
                wests = [column(0) * jnp.exp(log_decay * (lane + 1.0))]
                easts = [column(1) * jnp.exp(log_decay * (LANES - lane))]
                for _ in range(tiles - 1):
                    wests.append(wests[-1] * hop)
                    easts.append(easts[-1] * hop)
                for c in range(tiles):
                    values = jnp.concatenate([ref[source, g * tiles + c] for g in range(groups)], 0)
                    high, low = split(values + (wests[c] + easts[tiles - 1 - c]))
                    cols = slice((part * tiles + c) * LANES, (part * tiles + c + 1) * LANES)
                    high_ref[source * lats : (source + 1) * lats, cols] = high
                    low_ref[source * lats : (source + 1) * lats, cols] = low

    k_high, k_low = split(kernel_ref[...])
    for part in range(2):
        cols = slice(part * tiles * LANES, (part + 1) * tiles * LANES)
        result = dot3(k_high, k_low, high_ref[:, cols], low_ref[:, cols])
        out_ref[:, part] = result.reshape(-1, lats, tiles * LANES)


def convolved(first, second, lat_kernel, lats, lons):
    sources = first.shape[0]
    nlat = sources * lats
    group = 4
    return pl.pallas_call(
        convolve_kernel,
        grid=(sources // group,),
        in_specs=[
            pl.BlockSpec(first.shape, lambda j: (0, 0, 0, 0)),
            pl.BlockSpec(second.shape, lambda j: (0, 0, 0, 0)),
            pl.BlockSpec((group * lats, nlat), lambda j: (j, 0)),
        ],
        out_specs=pl.BlockSpec((group, 2, lats, lons), lambda j: (j, 0, 0, 0)),
        out_shape=jax.ShapeDtypeStruct((sources, 2, lats, lons), jnp.float32),
        scratch_shapes=[
            pltpu.VMEM((nlat, 2 * lons), jnp.bfloat16),
            pltpu.VMEM((nlat, 2 * lons), jnp.bfloat16),
        ],
        cost_estimate=pl.CostEstimate(flops=28 * 10**8, bytes_accessed=8 * 10**6, transcendentals=4 * 10**5),
        name="convolve",
    )(first, second, lat_kernel)


def on_device(field, vertical, rate, lat_kernel):
    ring = lax.axis_size("lon")
    levels, lats, lons = field.shape

    def to_owner(v):
        return lax.all_to_all(v, "lat", 0, 0, tiled=True)

    first, edge = filtered_blocks(0, field, vertical, rate)
    first = to_owner(first)
    second, edge = filtered_blocks(1, field, vertical, rate, (edge,))
    hops = [edge] + [lax.ppermute(edge, "lon", [(i, (i + hop) % ring) for i in range(ring)]) for hop in range(1, ring)]
    second = to_owner(with_states(lons, rate, hops, second))
    out = convolved(first, second, lat_kernel, lats, lons)
    return to_owner(out).reshape(levels, lats, lons)


def solution(mesh):
    return jax.shard_map(
        on_device,
        mesh=mesh,
        in_specs=(P(None, "lat", "lon"), P(), P(None, "lat"), P()),
        out_specs=P(None, "lat", "lon"),
        check_vma=False,
    )
```

```python
import functools

import jax
import jax.numpy as jnp
from jax import lax
from jax.experimental import pallas as pl
from jax.experimental.pallas import tpu as pltpu
from jax.sharding import PartitionSpec as P

LANES = 128
SUB = 8
MID = LANES // 2


def split(x):
    high = x.astype(jnp.bfloat16)
    return high, (x - high.astype(jnp.float32)).astype(jnp.bfloat16)


def dot(a, b):
    return jnp.dot(a, b, preferred_element_type=jnp.float32)


def dot3(a_high, a_low, b_high, b_low):
    return dot(a_high, b_high) + (dot(a_high, b_low) + dot(a_low, b_high))


def iota(shape, dim):
    return lax.broadcasted_iota(jnp.int32, shape, dim)


def log_decays(rate):
    decay = 1.0 - rate
    gap = decay - 1.0
    return jnp.log(decay) * (rate / -gap)


def columns(tile, levels):
    return jnp.concatenate([jnp.broadcast_to(tile[:, k : k + 1], (SUB, LANES)) for k in range(levels)], 0)


def filter_kernel(field_hbm, vertical_hbm, rate_hbm, out_ref, edge_ref, decay_ref, turned_ref, field_ref, vertical_ref, rate_ref, matrix_ref, sums_ref, edges_ref, sems):
    groups, levels, _, lons = field_ref.shape
    rows = levels * SUB
    lats = groups * SUB
    tiles = lons // LANES
    small = [
        pltpu.make_async_copy(rate_hbm, rate_ref, sems.at[groups]),
        pltpu.make_async_copy(vertical_hbm, vertical_ref, sems.at[groups + 1]),
    ]
    for copy in small:
        copy.start()
    copies = [pltpu.make_async_copy(field_hbm.at[:, pl.ds(g * SUB, SUB), :], field_ref.at[g], sems.at[g]) for g in range(groups)]
    for copy in copies:
        copy.start()
    spread = (iota((rows, levels), 0) // SUB == iota((rows, levels), 1)).astype(jnp.bfloat16)
    across = (iota((levels, rows), 1) // SUB == iota((levels, rows), 0)).astype(jnp.bfloat16)
    same = iota((rows, rows), 0) % SUB == iota((rows, rows), 1) % SUB
    source, target = iota((2 * LANES, 2 * LANES), 0) % LANES, iota((2 * LANES, 2 * LANES), 1)
    sums_ref[0] = ((source <= target) | (target >= LANES)).astype(jnp.bfloat16)
    sums_ref[1] = ((source > target) | (target >= LANES)).astype(jnp.bfloat16)
    edges_ref[...] = jnp.zeros_like(edges_ref)
    small[0].wait()
    filled = jnp.full((levels, MID - lats), 0.5, jnp.float32)
    rate = rate_ref[...]
    rate = jnp.concatenate([rate, filled, rate, filled], 1)
    rest = jnp.zeros((LANES - levels, LANES), jnp.float32)
    log_decay = log_decays(rate)
    decay_ref[...] = log_decay
    turned_ref[0] = jnp.concatenate([log_decay, rest], 0).T
    turned_ref[1] = jnp.concatenate([rate / (2.0 - rate), rest], 0).T
    small[1].wait()
    for i, piece in enumerate(split(vertical_ref[...])):
        tall = dot(spread, piece).astype(jnp.bfloat16)
        matrix_ref[i] = jnp.where(same, dot(tall, across), 0.0).astype(jnp.bfloat16)

    narrow = iota((SUB, LANES), 1)
    offset = (iota((rows, LANES), 1) - MID).astype(jnp.float32)
    for g in range(groups):
        if g % 3 == 0:
            for copy in copies[g : g + 3]:
                copy.wait()
        x_high, x_low = split(field_ref[g].reshape(rows, lons))
        mixed = dot3(matrix_ref[0], matrix_ref[1], x_high, x_low)
        here = slice(g * SUB, (g + 1) * SUB)
        log_decay, gain = columns(turned_ref[0, here], levels), columns(turned_ref[1, here], levels)
        falling, rising = jnp.exp(offset * log_decay), jnp.exp(-offset * log_decay)
        half = jnp.exp(MID * log_decay)

        def summed(scale, sums):
            pieces = [jnp.concatenate(split(mixed[:, c * LANES : (c + 1) * LANES] * scale), 1) for c in range(tiles)]
            both = dot(jnp.concatenate(pieces, 0), sums)
            return [both[c * rows : (c + 1) * rows, :LANES] for c in range(tiles)], [both[c * rows : (c + 1) * rows, LANES:] for c in range(tiles)]

        east, all_east = summed(rising * gain, sums_ref[0])
        west, all_west = summed(falling * gain, sums_ref[1])
        carry = 0.0
        for c in range(tiles):
            east[c] = east[c] + carry
            last = half * (all_east[c] + carry)
            carry = half * last
        carry = 0.0
        for c in range(tiles - 1, -1, -1):
            west[c] = west[c] + carry
            first = half * (all_west[c] + carry)
            carry = half * first
        for c in range(tiles):
            total = falling * east[c] + rising * west[c]
            out_ref[:, :, g * tiles + c] = total.reshape(levels // 2, 2, SUB, LANES)
        for value, base in ((last, 0), (first, MID)):
            edges = jnp.zeros((SUB, LANES), jnp.float32)
            for k in range(levels):
                edges = jnp.where(narrow == k, value[k * SUB : (k + 1) * SUB], edges)
            edges_ref[base + g * SUB : base + (g + 1) * SUB, :] = edges
    edge_ref[...] = jnp.broadcast_to(edges_ref[...].T[None, :levels], edge_ref.shape)


HBM = pl.BlockSpec(memory_space=pltpu.HBM)
VMEM = pl.BlockSpec(memory_space=pltpu.VMEM)


def filtered_blocks(ring, field, vertical, rate):
    levels, lats, lons = field.shape
    groups, rows, tiles = lats // SUB, levels * SUB, lons // LANES
    return pl.pallas_call(
        filter_kernel,
        in_specs=[HBM] * 3,
        out_specs=[VMEM] * 4,
        out_shape=[
            jax.ShapeDtypeStruct((levels // 2, 2, groups * tiles, SUB, LANES), jnp.float32),
            jax.ShapeDtypeStruct((ring, levels, LANES), jnp.float32),
            jax.ShapeDtypeStruct((levels, LANES), jnp.float32),
            jax.ShapeDtypeStruct((2, LANES, LANES), jnp.float32),
        ],
        scratch_shapes=[
            pltpu.VMEM((groups, levels, SUB, lons), jnp.float32),
            pltpu.VMEM(vertical.shape, jnp.float32),
            pltpu.VMEM(rate.shape, jnp.float32),
            pltpu.VMEM((2, rows, rows), jnp.bfloat16),
            pltpu.VMEM((2, 2 * LANES, 2 * LANES), jnp.bfloat16),
            pltpu.VMEM((LANES, LANES), jnp.float32),
            pltpu.SemaphoreType.DMA((groups + 2,)),
        ],
        compiler_params=pltpu.CompilerParams(vmem_limit_bytes=16 << 20),
        cost_estimate=pl.CostEstimate(flops=16 * 10**8, bytes_accessed=5 * 10**6, transcendentals=2 * 10**5),
        name="mix_filter",
    )(*[pltpu.with_memory_space_constraint(v, pltpu.HBM) for v in (field, vertical, rate)])


def add_states_kernel(width, place_ref, decay_ref, turned_ref, edge_ref, values_ref, out_ref, state_ref):
    ring, levels, _ = edge_ref.shape
    tiles = width // LANES
    groups = out_ref.shape[2] // tiles
    rows = levels * SUB
    log_decay = decay_ref[...]
    eastward = iota((levels, LANES), 1) < MID
    total = jnp.zeros((levels, LANES), jnp.float32)
    for device in range(ring):
        away = (place_ref[0] + ring - device) % ring
        blocks = jnp.where(eastward, (away + ring - 1) % ring, ring - 1 - away).astype(jnp.float32)
        total = total + edge_ref[device] * jnp.exp(blocks * (width * log_decay))
    total = total / (1.0 - jnp.exp((ring * width) * log_decay))
    state_ref[...] = jnp.concatenate([total, jnp.zeros((LANES - levels, LANES), jnp.float32)], 0).T
    lane = iota((rows, LANES), 1).astype(jnp.float32)
    for g in range(groups):
        log_decay = columns(turned_ref[0, g * SUB : (g + 1) * SUB], levels)
        hop = jnp.exp(float(LANES) * log_decay)
        wests = [columns(state_ref[g * SUB : (g + 1) * SUB], levels) * jnp.exp(log_decay * lane)]
        easts = [columns(state_ref[MID + g * SUB : MID + (g + 1) * SUB], levels) * jnp.exp(log_decay * (LANES - lane))]
        for _ in range(tiles - 1):
            wests.append(wests[-1] * hop)
            easts.append(easts[-1] * hop)
        for c in range(tiles):
            more = wests[c] + easts[tiles - 1 - c]
            out_ref[:, :, g * tiles + c] = values_ref[:, :, g * tiles + c] + more.reshape(levels // 2, 2, SUB, LANES)


def with_states(width, where, decay, turned, edges, values):
    return pl.pallas_call(
        functools.partial(add_states_kernel, width),
        in_specs=[pl.BlockSpec(memory_space=pltpu.SMEM)] + [VMEM] * 4,
        out_specs=VMEM,
        out_shape=jax.ShapeDtypeStruct(values.shape, values.dtype),
        scratch_shapes=[pltpu.VMEM((LANES, LANES), jnp.float32)],
        input_output_aliases={4: 0},
        compiler_params=pltpu.CompilerParams(vmem_limit_bytes=16 << 20),
        cost_estimate=pl.CostEstimate(flops=10**7, bytes_accessed=5 * 10**6, transcendentals=10**5),
        name="add_states",
    )(where, decay, turned, edges, values)


def convolve_kernel(values_ref, kernel_ref, out_ref, high_ref, low_ref):
    sources, parts, lats, lons = out_ref.shape
    tiles = lons // LANES
    groups = lats // SUB
    for part in range(parts):
        for source in range(sources):
            rows = slice(source * lats, (source + 1) * lats)
            for c in range(tiles):
                values = jnp.concatenate([values_ref[source, part, g * tiles + c] for g in range(groups)], 0)
                cols = slice((part * tiles + c) * LANES, (part * tiles + c + 1) * LANES)
                high_ref[rows, cols], low_ref[rows, cols] = split(values)
    group = 4
    for j in range(0, sources, group):
        k_high, k_low = split(kernel_ref[j * lats : (j + group) * lats])
        for part in range(parts):
            cols = slice(part * lons, (part + 1) * lons)
            result = dot3(k_high, k_low, high_ref[:, cols], low_ref[:, cols])
            out_ref[j : j + group, part] = result.reshape(group, lats, lons)


def convolved(values, lat_kernel, lats, lons):
    sources = values.shape[0]
    nlat = sources * lats
    return pl.pallas_call(
        convolve_kernel,
        in_specs=[VMEM] * 2,
        out_specs=VMEM,
        out_shape=jax.ShapeDtypeStruct((sources, 2, lats, lons), jnp.float32),
        scratch_shapes=[
            pltpu.VMEM((nlat, 2 * lons), jnp.bfloat16),
            pltpu.VMEM((nlat, 2 * lons), jnp.bfloat16),
        ],
        compiler_params=pltpu.CompilerParams(vmem_limit_bytes=16 << 20),
        cost_estimate=pl.CostEstimate(flops=28 * 10**8, bytes_accessed=8 * 10**6, transcendentals=0),
        name="convolve",
    )(values, lat_kernel)


def in_place(v):
    return pl.pallas_call(
        lambda v_ref, out_ref: None,
        in_specs=[HBM],
        out_specs=HBM,
        out_shape=jax.ShapeDtypeStruct(v.shape, v.dtype),
        input_output_aliases={0: 0},
        compiler_params=pltpu.CompilerParams(vmem_limit_bytes=1 << 20),
        name="in_place",
    )(pltpu.with_memory_space_constraint(v, pltpu.HBM))


def on_device(field, vertical, rate, lat_kernel):
    ring = lax.axis_size("lon")
    levels, lats, lons = field.shape
    where = lax.axis_index("lon").reshape(1)

    def exchanged(v, axis):
        return lax.all_to_all(v, axis, 0, 0, tiled=True)

    values, edges, decay, turned = filtered_blocks(ring, field, vertical, rate)
    where, edges = lax.optimization_barrier((where, edges))
    values = with_states(lons, where, decay, turned, exchanged(edges, "lon"), values)
    out = convolved(exchanged(values, "lat"), lat_kernel, lats, lons)
    return exchanged(out, "lat").reshape(levels, lats, lons)


def solution(mesh):
    return jax.shard_map(
        on_device,
        mesh=mesh,
        in_specs=(P(None, "lat", "lon"), P(), P(None, "lat"), P()),
        out_specs=P(None, "lat", "lon"),
        check_vma=False,
    )
```

```python
import functools

import jax
import jax.numpy as jnp
from jax import lax
from jax.experimental import pallas as pl
from jax.experimental.pallas import tpu as pltpu
from jax.sharding import PartitionSpec as P

LANES = 128
SUB = 8
MID = LANES // 2


def split(x):
    high = x.astype(jnp.bfloat16)
    return high, (x - high.astype(jnp.float32)).astype(jnp.bfloat16)


def dot(a, b):
    return jnp.dot(a, b, preferred_element_type=jnp.float32)


def dot3(a_high, a_low, b_high, b_low):
    return dot(a_high, b_high) + (dot(a_high, b_low) + dot(a_low, b_high))


def iota(shape, dim):
    return lax.broadcasted_iota(jnp.int32, shape, dim)


def log_decays(rate):
    decay = 1.0 - rate
    gap = decay - 1.0
    return jnp.log(decay) * (rate / -gap)


def columns(tile, levels):
    return jnp.concatenate([jnp.broadcast_to(tile[:, k : k + 1], (SUB, LANES)) for k in range(levels)], 0)


def mix_kernel(batch, field_hbm, vertical_hbm, rate_hbm, mixed_ref, edge_ref, decay_ref, turned_ref, field_ref, vertical_ref, rate_ref, matrix_ref, edges_ref, sems):
    groups, rows, lons = mixed_ref.shape
    levels = rows // SUB
    lats = groups * SUB
    tiles = lons // LANES
    small = [
        pltpu.make_async_copy(rate_hbm, rate_ref, sems.at[groups]),
        pltpu.make_async_copy(vertical_hbm, vertical_ref, sems.at[groups + 1]),
    ]
    for copy in small:
        copy.start()
    copies = [pltpu.make_async_copy(field_hbm.at[:, pl.ds(g * SUB, SUB), :], field_ref.at[g], sems.at[g]) for g in range(groups)]
    for copy in copies:
        copy.start()
    spread = (iota((rows, levels), 0) // SUB == iota((rows, levels), 1)).astype(jnp.bfloat16)
    across = (iota((levels, rows), 1) // SUB == iota((levels, rows), 0)).astype(jnp.bfloat16)
    same = iota((rows, rows), 0) % SUB == iota((rows, rows), 1) % SUB
    ones = jnp.ones((2 * LANES, LANES), jnp.bfloat16)
    edges_ref[...] = jnp.zeros_like(edges_ref)
    small[0].wait()
    filled = jnp.full((levels, MID - lats), 0.5, jnp.float32)
    rate = rate_ref[...]
    rate = jnp.concatenate([rate, filled, rate, filled], 1)
    rest = jnp.zeros((LANES - levels, LANES), jnp.float32)
    log_decay = log_decays(rate)
    decay_ref[...] = log_decay
    turned_ref[0] = jnp.concatenate([log_decay, rest], 0).T
    turned_ref[1] = jnp.concatenate([rate / (2.0 - rate), rest], 0).T
    small[1].wait()
    for i, piece in enumerate(split(vertical_ref[...])):
        tall = dot(spread, piece).astype(jnp.bfloat16)
        matrix_ref[i] = jnp.where(same, dot(tall, across), 0.0).astype(jnp.bfloat16)

    lane = iota((rows, LANES), 1).astype(jnp.float32)
    narrow = iota((SUB, LANES), 1)
    for first_group in range(0, groups, batch):
        batched = range(first_group, first_group + batch)
        for g in batched:
            copies[g].wait()
        x_high, x_low = split(jnp.concatenate([field_ref[g].reshape(rows, lons) for g in batched], 1))
        mixed_batch = dot3(matrix_ref[0], matrix_ref[1], x_high, x_low)
        for at, g in enumerate(batched):
            mixed = mixed_batch[:, at * lons : (at + 1) * lons]
            mixed_ref[g] = mixed
            value = [mixed[:, c * LANES : (c + 1) * LANES] for c in range(tiles)]
            here = slice(g * SUB, (g + 1) * SUB)
            log_decay = columns(turned_ref[0, here], levels)
            hop = jnp.exp(float(LANES) * log_decay)
            last, first = value[0], value[-1]
            for c in range(1, tiles):
                last = last * hop + value[c]
                first = first * hop + value[tiles - 1 - c]
            last = last * jnp.exp((LANES - lane) * log_decay)
            first = first * jnp.exp(lane * log_decay)
            for weighted, base in ((last, 0), (first, MID)):
                total = dot(jnp.concatenate(split(weighted), 1), ones)
                edges = jnp.zeros((SUB, LANES), jnp.float32)
                for k in range(levels):
                    edges = jnp.where(narrow == k, total[k * SUB : (k + 1) * SUB], edges)
                edges_ref[base + g * SUB : base + (g + 1) * SUB, :] = edges * turned_ref[1, here]
    edge_ref[...] = jnp.broadcast_to(edges_ref[...].T[None, :levels], edge_ref.shape)


HBM = pl.BlockSpec(memory_space=pltpu.HBM)
VMEM = pl.BlockSpec(memory_space=pltpu.VMEM)


def mixed_levels(ring, field, vertical, rate):
    levels, lats, lons = field.shape
    groups, rows = lats // SUB, levels * SUB
    return pl.pallas_call(
        functools.partial(mix_kernel, 2 if groups % 2 == 0 else 1),
        in_specs=[HBM] * 3,
        out_specs=[VMEM] * 4,
        out_shape=[
            jax.ShapeDtypeStruct((groups, rows, lons), jnp.float32),
            jax.ShapeDtypeStruct((ring, levels, LANES), jnp.float32),
            jax.ShapeDtypeStruct((levels, LANES), jnp.float32),
            jax.ShapeDtypeStruct((2, LANES, LANES), jnp.float32),
        ],
        scratch_shapes=[
            pltpu.VMEM((groups, levels, SUB, lons), jnp.float32),
            pltpu.VMEM(vertical.shape, jnp.float32),
            pltpu.VMEM(rate.shape, jnp.float32),
            pltpu.VMEM((2, rows, rows), jnp.bfloat16),
            pltpu.VMEM((LANES, LANES), jnp.float32),
            pltpu.SemaphoreType.DMA((groups + 2,)),
        ],
        compiler_params=pltpu.CompilerParams(vmem_limit_bytes=16 << 20),
        cost_estimate=pl.CostEstimate(flops=8 * 10**8, bytes_accessed=5 * 10**6, transcendentals=2 * 10**5),
        name="mix",
    )(*[pltpu.with_memory_space_constraint(v, pltpu.HBM) for v in (field, vertical, rate)])


def filter_kernel(place_ref, decay_ref, turned_ref, edge_ref, mixed_ref, out_ref, state_ref):
    groups, rows, lons = mixed_ref.shape
    ring, levels, _ = edge_ref.shape
    tiles = lons // LANES
    log_decay = decay_ref[...]
    eastward = iota((levels, LANES), 1) < MID
    total = jnp.zeros((levels, LANES), jnp.float32)
    for device in range(ring):
        away = (place_ref[0] + ring - device) % ring
        blocks = jnp.where(eastward, (away + ring - 1) % ring, ring - 1 - away).astype(jnp.float32)
        total = total + edge_ref[device] * jnp.exp(blocks * (lons * log_decay))
    total = total / (1.0 - jnp.exp((ring * lons) * log_decay))
    state_ref[...] = jnp.concatenate([total, jnp.zeros((LANES - levels, LANES), jnp.float32)], 0).T
    source, target = iota((2 * LANES, 2 * LANES), 0) % LANES, iota((2 * LANES, 2 * LANES), 1)
    sums_east = ((source <= target) | (target >= LANES)).astype(jnp.bfloat16)
    sums_west = ((source > target) | (target >= LANES)).astype(jnp.bfloat16)
    offset = (iota((rows, LANES), 1) - MID).astype(jnp.float32)
    for g in range(groups):
        here = slice(g * SUB, (g + 1) * SUB)
        log_decay, gain = columns(turned_ref[0, here], levels), columns(turned_ref[1, here], levels)
        falling, rising = jnp.exp(offset * log_decay), jnp.exp(-offset * log_decay)
        half = jnp.exp(MID * log_decay)

        def summed(scale, sums):
            pieces = [jnp.concatenate(split(mixed_ref[g, :, c * LANES : (c + 1) * LANES] * scale), 1) for c in range(tiles)]
            both = dot(jnp.concatenate(pieces, 0), sums)
            return [both[c * rows : (c + 1) * rows, :LANES] for c in range(tiles)], [both[c * rows : (c + 1) * rows, LANES:] for c in range(tiles)]

        east, all_east = summed(rising * gain, sums_east)
        west, all_west = summed(falling * gain, sums_west)
        carry = half * columns(state_ref[g * SUB : (g + 1) * SUB], levels)
        for c in range(tiles):
            east[c] = east[c] + carry
            carry = half * (half * (all_east[c] + carry))
        carry = half * columns(state_ref[MID + g * SUB : MID + (g + 1) * SUB], levels)
        for c in range(tiles - 1, -1, -1):
            west[c] = west[c] + carry
            carry = half * (half * (all_west[c] + carry))
        for c in range(tiles):
            filtered = falling * east[c] + rising * west[c]
            out_ref[:, :, g * tiles + c] = filtered.reshape(levels // 2, 2, SUB, LANES)


def filtered_blocks(where, decay, turned, edges, mixed):
    groups, rows, lons = mixed.shape
    levels, tiles = rows // SUB, lons // LANES
    return pl.pallas_call(
        filter_kernel,
        in_specs=[pl.BlockSpec(memory_space=pltpu.SMEM)] + [VMEM] * 4,
        out_specs=VMEM,
        out_shape=jax.ShapeDtypeStruct((levels // 2, 2, groups * tiles, SUB, LANES), jnp.float32),
        scratch_shapes=[pltpu.VMEM((LANES, LANES), jnp.float32)],
        compiler_params=pltpu.CompilerParams(vmem_limit_bytes=16 << 20),
        cost_estimate=pl.CostEstimate(flops=8 * 10**8, bytes_accessed=5 * 10**6, transcendentals=2 * 10**5),
        name="filter",
    )(where, decay, turned, edges, mixed)


def convolve_kernel(values_ref, kernel_ref, out_ref, high_ref, low_ref):
    sources, parts, lats, lons = out_ref.shape
    tiles = lons // LANES
    groups = lats // SUB
    for part in range(parts):
        for source in range(sources):
            rows = slice(source * lats, (source + 1) * lats)
            for c in range(tiles):
                values = jnp.concatenate([values_ref[source, part, g * tiles + c] for g in range(groups)], 0)
                cols = slice((part * tiles + c) * LANES, (part * tiles + c + 1) * LANES)
                high_ref[rows, cols], low_ref[rows, cols] = split(values)
    group = 4
    for j in range(0, sources, group):
        k_high, k_low = split(kernel_ref[j * lats : (j + group) * lats])
        result = dot3(k_high, k_low, high_ref[...], low_ref[...])
        for part in range(parts):
            out_ref[j : j + group, part] = result[:, part * lons : (part + 1) * lons].reshape(group, lats, lons)


def convolved(values, lat_kernel, lats, lons):
    sources = values.shape[0]
    nlat = sources * lats
    return pl.pallas_call(
        convolve_kernel,
        in_specs=[VMEM] * 2,
        out_specs=VMEM,
        out_shape=jax.ShapeDtypeStruct((sources, 2, lats, lons), jnp.float32),
        scratch_shapes=[
            pltpu.VMEM((nlat, 2 * lons), jnp.bfloat16),
            pltpu.VMEM((nlat, 2 * lons), jnp.bfloat16),
        ],
        compiler_params=pltpu.CompilerParams(vmem_limit_bytes=16 << 20),
        cost_estimate=pl.CostEstimate(flops=28 * 10**8, bytes_accessed=8 * 10**6, transcendentals=0),
        name="convolve",
    )(values, lat_kernel)


def on_device(field, vertical, rate, lat_kernel):
    ring = lax.axis_size("lon")
    levels, lats, lons = field.shape
    where = lax.axis_index("lon").reshape(1)

    def exchanged(v, axis):
        return lax.all_to_all(v, axis, 0, 0, tiled=True)

    mixed, edges, decay, turned = mixed_levels(ring, field, vertical, rate)
    where, edges = lax.optimization_barrier((where, edges))
    values = filtered_blocks(where, decay, turned, exchanged(edges, "lon"), mixed)
    out = convolved(exchanged(values, "lat"), lat_kernel, lats, lons)
    return exchanged(out, "lat").reshape(levels, lats, lons)


def solution(mesh):
    return jax.shard_map(
        on_device,
        mesh=mesh,
        in_specs=(P(None, "lat", "lon"), P(), P(None, "lat"), P()),
        out_specs=P(None, "lat", "lon"),
        check_vma=False,
    )
```

```python
import functools

import jax
import jax.numpy as jnp
from jax import lax
from jax.experimental import pallas as pl
from jax.experimental.pallas import tpu as pltpu
from jax.sharding import PartitionSpec as P

LANES = 128
SUB = 8
MID = LANES // 2


def split(x):
    high = x.astype(jnp.bfloat16)
    return high, (x - high.astype(jnp.float32)).astype(jnp.bfloat16)


def dot(a, b):
    return jnp.dot(a, b, preferred_element_type=jnp.float32)


def dot3(a_high, a_low, b_high, b_low):
    return dot(a_high, b_high) + (dot(a_high, b_low) + dot(a_low, b_high))


def iota(shape, dim):
    return lax.broadcasted_iota(jnp.int32, shape, dim)


def log_decays(rate):
    decay = 1.0 - rate
    gap = decay - 1.0
    return jnp.log(decay) * (rate / -gap)


def columns(tile, levels):
    return jnp.concatenate([jnp.broadcast_to(tile[:, k : k + 1], (SUB, LANES)) for k in range(levels)], 0)


def mix_kernel(batch, field_hbm, vertical_hbm, rate_hbm, mixed_ref, edge_ref, decay_ref, turned_ref, field_ref, vertical_ref, rate_ref, matrix_ref, edges_ref, sems):
    groups, rows, lons = mixed_ref.shape
    levels = rows // SUB
    lats = groups * SUB
    tiles = lons // LANES
    small = [
        pltpu.make_async_copy(rate_hbm, rate_ref, sems.at[groups]),
        pltpu.make_async_copy(vertical_hbm, vertical_ref, sems.at[groups + 1]),
    ]
    for copy in small:
        copy.start()
    copies = [pltpu.make_async_copy(field_hbm.at[:, pl.ds(g * SUB, SUB), :], field_ref.at[g], sems.at[g]) for g in range(groups)]
    for copy in copies:
        copy.start()
    spread = (iota((rows, levels), 0) // SUB == iota((rows, levels), 1)).astype(jnp.bfloat16)
    across = (iota((levels, rows), 1) // SUB == iota((levels, rows), 0)).astype(jnp.bfloat16)
    same = iota((rows, rows), 0) % SUB == iota((rows, rows), 1) % SUB
    ones = jnp.ones((2 * LANES, LANES), jnp.bfloat16)
    edges_ref[...] = jnp.zeros_like(edges_ref)
    small[0].wait()
    filled = jnp.full((levels, MID - lats), 0.5, jnp.float32)
    rate = rate_ref[...]
    rate = jnp.concatenate([rate, filled, rate, filled], 1)
    rest = jnp.zeros((LANES - levels, LANES), jnp.float32)
    log_decay = log_decays(rate)
    decay_ref[...] = log_decay
    turned_ref[0] = jnp.concatenate([log_decay, rest], 0).T
    turned_ref[1] = jnp.concatenate([rate / (2.0 - rate), rest], 0).T
    small[1].wait()
    for i, piece in enumerate(split(vertical_ref[...])):
        tall = dot(spread, piece).astype(jnp.bfloat16)
        matrix_ref[i] = jnp.where(same, dot(tall, across), 0.0).astype(jnp.bfloat16)

    lane = iota((rows, LANES), 1).astype(jnp.float32)
    narrow = iota((SUB, LANES), 1)
    for first_group in range(0, groups, batch):
        batched = range(first_group, first_group + batch)
        for g in batched:
            copies[g].wait()
        x_high, x_low = split(jnp.concatenate([field_ref[g].reshape(rows, lons) for g in batched], 1))
        mixed_batch = dot3(matrix_ref[0], matrix_ref[1], x_high, x_low)
        for at, g in enumerate(batched):
            mixed = mixed_batch[:, at * lons : (at + 1) * lons]
            mixed_ref[g] = mixed
            value = [mixed[:, c * LANES : (c + 1) * LANES] for c in range(tiles)]
            here = slice(g * SUB, (g + 1) * SUB)
            log_decay = columns(turned_ref[0, here], levels)
            hop = jnp.exp(float(LANES) * log_decay)
            last, first = value[0], value[-1]
            for c in range(1, tiles):
                last = last * hop + value[c]
                first = first * hop + value[tiles - 1 - c]
            last = last * jnp.exp((LANES - lane) * log_decay)
            first = first * jnp.exp(lane * log_decay)
            for weighted, base in ((last, 0), (first, MID)):
                total = dot(jnp.concatenate(split(weighted), 1), ones)
                edges = jnp.zeros((SUB, LANES), jnp.float32)
                for k in range(levels):
                    edges = jnp.where(narrow == k, total[k * SUB : (k + 1) * SUB], edges)
                edges_ref[base + g * SUB : base + (g + 1) * SUB, :] = edges * turned_ref[1, here]
    edge_ref[...] = jnp.broadcast_to(edges_ref[...].T[None, :levels], edge_ref.shape)


HBM = pl.BlockSpec(memory_space=pltpu.HBM)
VMEM = pl.BlockSpec(memory_space=pltpu.VMEM)


def mixed_levels(ring, field, vertical, rate):
    levels, lats, lons = field.shape
    groups, rows = lats // SUB, levels * SUB
    return pl.pallas_call(
        functools.partial(mix_kernel, groups),
        in_specs=[HBM] * 3,
        out_specs=[VMEM] * 4,
        out_shape=[
            jax.ShapeDtypeStruct((groups, rows, lons), jnp.float32),
            jax.ShapeDtypeStruct((ring, levels, LANES), jnp.float32),
            jax.ShapeDtypeStruct((levels, LANES), jnp.float32),
            jax.ShapeDtypeStruct((2, LANES, LANES), jnp.float32),
        ],
        scratch_shapes=[
            pltpu.VMEM((groups, levels, SUB, lons), jnp.float32),
            pltpu.VMEM(vertical.shape, jnp.float32),
            pltpu.VMEM(rate.shape, jnp.float32),
            pltpu.VMEM((2, rows, rows), jnp.bfloat16),
            pltpu.VMEM((LANES, LANES), jnp.float32),
            pltpu.SemaphoreType.DMA((groups + 2,)),
        ],
        compiler_params=pltpu.CompilerParams(vmem_limit_bytes=16 << 20),
        cost_estimate=pl.CostEstimate(flops=8 * 10**8, bytes_accessed=5 * 10**6, transcendentals=2 * 10**5),
        name="mix",
    )(*[pltpu.with_memory_space_constraint(v, pltpu.HBM) for v in (field, vertical, rate)])


def filter_kernel(batch, place_ref, decay_ref, turned_ref, edge_ref, mixed_ref, out_ref, state_ref):
    groups, rows, lons = mixed_ref.shape
    ring, levels, _ = edge_ref.shape
    tiles = lons // LANES
    log_decay = decay_ref[...]
    eastward = iota((levels, LANES), 1) < MID
    total = jnp.zeros((levels, LANES), jnp.float32)
    for device in range(ring):
        away = (place_ref[0] + ring - device) % ring
        blocks = jnp.where(eastward, (away + ring - 1) % ring, ring - 1 - away).astype(jnp.float32)
        total = total + edge_ref[device] * jnp.exp(blocks * (lons * log_decay))
    total = total / (1.0 - jnp.exp((ring * lons) * log_decay))
    state_ref[...] = jnp.concatenate([total, jnp.zeros((LANES - levels, LANES), jnp.float32)], 0).T
    source, target = iota((2 * LANES, 2 * LANES), 0) % LANES, iota((2 * LANES, 2 * LANES), 1)
    sums_east = ((source <= target) | (target >= LANES)).astype(jnp.bfloat16)
    sums_west = ((source > target) | (target >= LANES)).astype(jnp.bfloat16)
    offset = (iota((rows, LANES), 1) - MID).astype(jnp.float32)
    for first_group in range(0, groups, batch):
        batched = range(first_group, first_group + batch)
        falling, rising, half, from_east, from_west = [], [], [], [], []
        for g in batched:
            here = slice(g * SUB, (g + 1) * SUB)
            log_decay, gain = columns(turned_ref[0, here], levels), columns(turned_ref[1, here], levels)
            falling.append(jnp.exp(offset * log_decay))
            rising.append(jnp.exp(-offset * log_decay))
            half.append(jnp.exp(MID * log_decay))
            for scale, pieces in ((rising[-1] * gain, from_east), (falling[-1] * gain, from_west)):
                pieces += [jnp.concatenate(split(mixed_ref[g, :, c * LANES : (c + 1) * LANES] * scale), 1) for c in range(tiles)]
        sums = [dot(jnp.concatenate(pieces, 0), table) for pieces, table in ((from_east, sums_east), (from_west, sums_west))]
        for at, g in enumerate(batched):
            east, west = ([s[(at * tiles + c) * rows : (at * tiles + c + 1) * rows] for c in range(tiles)] for s in sums)
            carry = half[at] * columns(state_ref[g * SUB : (g + 1) * SUB], levels)
            for c in range(tiles):
                onward = half[at] * (half[at] * (east[c][:, LANES:] + carry))
                east[c] = east[c][:, :LANES] + carry
                carry = onward
            carry = half[at] * columns(state_ref[MID + g * SUB : MID + (g + 1) * SUB], levels)
            for c in range(tiles - 1, -1, -1):
                onward = half[at] * (half[at] * (west[c][:, LANES:] + carry))
                west[c] = west[c][:, :LANES] + carry
                carry = onward
            for c in range(tiles):
                filtered = falling[at] * east[c] + rising[at] * west[c]
                out_ref[:, :, g * tiles + c] = filtered.reshape(levels // 2, 2, SUB, LANES)


def filtered_blocks(where, decay, turned, edges, mixed):
    groups, rows, lons = mixed.shape
    levels, tiles = rows // SUB, lons // LANES
    return pl.pallas_call(
        functools.partial(filter_kernel, groups),
        in_specs=[pl.BlockSpec(memory_space=pltpu.SMEM)] + [VMEM] * 4,
        out_specs=VMEM,
        out_shape=jax.ShapeDtypeStruct((levels // 2, 2, groups * tiles, SUB, LANES), jnp.float32),
        scratch_shapes=[pltpu.VMEM((LANES, LANES), jnp.float32)],
        compiler_params=pltpu.CompilerParams(vmem_limit_bytes=16 << 20),
        cost_estimate=pl.CostEstimate(flops=8 * 10**8, bytes_accessed=5 * 10**6, transcendentals=2 * 10**5),
        name="filter",
    )(where, decay, turned, edges, mixed)


def convolve_kernel(values_ref, kernel_ref, out_ref, high_ref, low_ref):
    sources, parts, lats, lons = out_ref.shape
    tiles = lons // LANES
    groups = lats // SUB
    for part in range(parts):
        for source in range(sources):
            rows = slice(source * lats, (source + 1) * lats)
            for c in range(tiles):
                values = jnp.concatenate([values_ref[source, part, g * tiles + c] for g in range(groups)], 0)
                cols = slice((part * tiles + c) * LANES, (part * tiles + c + 1) * LANES)
                high_ref[rows, cols], low_ref[rows, cols] = split(values)
    group = 4
    for j in range(0, sources, group):
        k_high, k_low = split(kernel_ref[j * lats : (j + group) * lats])
        result = dot3(k_high, k_low, high_ref[...], low_ref[...])
        for part in range(parts):
            out_ref[j : j + group, part] = result[:, part * lons : (part + 1) * lons].reshape(group, lats, lons)


def convolved(values, lat_kernel, lats, lons):
    sources = values.shape[0]
    nlat = sources * lats
    return pl.pallas_call(
        convolve_kernel,
        in_specs=[VMEM] * 2,
        out_specs=VMEM,
        out_shape=jax.ShapeDtypeStruct((sources, 2, lats, lons), jnp.float32),
        scratch_shapes=[
            pltpu.VMEM((nlat, 2 * lons), jnp.bfloat16),
            pltpu.VMEM((nlat, 2 * lons), jnp.bfloat16),
        ],
        compiler_params=pltpu.CompilerParams(vmem_limit_bytes=16 << 20),
        cost_estimate=pl.CostEstimate(flops=28 * 10**8, bytes_accessed=8 * 10**6, transcendentals=0),
        name="convolve",
    )(values, lat_kernel)


def on_device(field, vertical, rate, lat_kernel):
    ring = lax.axis_size("lon")
    levels, lats, lons = field.shape
    where = lax.axis_index("lon").reshape(1)

    def exchanged(v, axis):
        return lax.all_to_all(v, axis, 0, 0, tiled=True)

    mixed, edges, decay, turned = mixed_levels(ring, field, vertical, rate)
    where, edges = lax.optimization_barrier((where, edges))
    values = filtered_blocks(where, decay, turned, exchanged(edges, "lon"), mixed)
    out = convolved(exchanged(values, "lat"), lat_kernel, lats, lons)
    return exchanged(out, "lat").reshape(levels, lats, lons)


def solution(mesh):
    return jax.shard_map(
        on_device,
        mesh=mesh,
        in_specs=(P(None, "lat", "lon"), P(), P(None, "lat"), P()),
        out_specs=P(None, "lat", "lon"),
        check_vma=False,
    )
```

```python
import functools

import jax
import jax.numpy as jnp
from jax import lax
from jax.experimental import pallas as pl
from jax.experimental.pallas import tpu as pltpu
from jax.sharding import PartitionSpec as P

LANES = 128
SUB = 8
MID = LANES // 2


def split(x):
    high = x.astype(jnp.bfloat16)
    return high, (x - high.astype(jnp.float32)).astype(jnp.bfloat16)


def dot(a, b):
    return jnp.dot(a, b, preferred_element_type=jnp.float32)


def dot3(a_high, a_low, b_high, b_low):
    return dot(a_high, b_high) + (dot(a_high, b_low) + dot(a_low, b_high))


def iota(shape, dim):
    return lax.broadcasted_iota(jnp.int32, shape, dim)


def log_decays(rate):
    decay = 1.0 - rate
    gap = decay - 1.0
    return jnp.log(decay) * (rate / -gap)


def columns(tile, levels):
    return jnp.concatenate([jnp.broadcast_to(tile[:, k : k + 1], (SUB, LANES)) for k in range(levels)], 0)


def mix_kernel(batch, field_hbm, vertical_hbm, rate_hbm, mixed_ref, edge_ref, decay_ref, turned_ref, field_ref, vertical_ref, rate_ref, matrix_ref, edges_ref, sems):
    groups, rows, lons = mixed_ref.shape
    levels = rows // SUB
    lats = groups * SUB
    tiles = lons // LANES
    small = [
        pltpu.make_async_copy(rate_hbm, rate_ref, sems.at[groups]),
        pltpu.make_async_copy(vertical_hbm, vertical_ref, sems.at[groups + 1]),
    ]
    for copy in small:
        copy.start()
    copies = [pltpu.make_async_copy(field_hbm.at[:, pl.ds(g * SUB, SUB), :], field_ref.at[g], sems.at[g]) for g in range(groups)]
    for copy in copies:
        copy.start()
    spread = (iota((rows, levels), 0) // SUB == iota((rows, levels), 1)).astype(jnp.bfloat16)
    across = (iota((levels, rows), 1) // SUB == iota((levels, rows), 0)).astype(jnp.bfloat16)
    same = iota((rows, rows), 0) % SUB == iota((rows, rows), 1) % SUB
    ones = jnp.ones((2 * LANES, LANES), jnp.bfloat16)
    edges_ref[...] = jnp.zeros_like(edges_ref)
    small[0].wait()
    filled = jnp.full((levels, MID - lats), 0.5, jnp.float32)
    rate = rate_ref[...]
    rate = jnp.concatenate([rate, filled, rate, filled], 1)
    rest = jnp.zeros((LANES - levels, LANES), jnp.float32)
    log_decay = log_decays(rate)
    decay_ref[...] = log_decay
    turned_ref[0] = jnp.concatenate([log_decay, rest], 0).T
    turned_ref[1] = jnp.concatenate([rate / (2.0 - rate), rest], 0).T
    small[1].wait()
    for i, piece in enumerate(split(vertical_ref[...])):
        tall = dot(spread, piece).astype(jnp.bfloat16)
        matrix_ref[i] = jnp.where(same, dot(tall, across), 0.0).astype(jnp.bfloat16)

    lane = iota((rows, LANES), 1).astype(jnp.float32)
    narrow = iota((SUB, LANES), 1)
    weighted = []
    for first_group in range(0, groups, batch):
        batched = range(first_group, first_group + batch)
        for g in batched:
            copies[g].wait()
        x_high, x_low = split(jnp.concatenate([field_ref[g].reshape(rows, lons) for g in batched], 1))
        mixed_batch = dot3(matrix_ref[0], matrix_ref[1], x_high, x_low)
        for at, g in enumerate(batched):
            mixed = mixed_batch[:, at * lons : (at + 1) * lons]
            mixed_ref[g] = mixed
            value = [mixed[:, c * LANES : (c + 1) * LANES] for c in range(tiles)]
            here = slice(g * SUB, (g + 1) * SUB)
            log_decay = columns(turned_ref[0, here], levels)
            hop = jnp.exp(float(LANES) * log_decay)
            last, first = value[0], value[-1]
            for c in range(1, tiles):
                last = last * hop + value[c]
                first = first * hop + value[tiles - 1 - c]
            last = last * jnp.exp((LANES - lane) * log_decay)
            first = first * jnp.exp(lane * log_decay)
            weighted += [(last, g * SUB, here), (first, MID + g * SUB, here)]
    totals = dot(jnp.concatenate([jnp.concatenate(split(v), 1) for v, _, _ in weighted], 0), ones)
    for i, (_, base, here) in enumerate(weighted):
        edges = jnp.zeros((SUB, LANES), jnp.float32)
        for k in range(levels):
            at = i * rows + k * SUB
            edges = jnp.where(narrow == k, totals[at : at + SUB], edges)
        edges_ref[base : base + SUB, :] = edges * turned_ref[1, here]
    edge_ref[...] = jnp.broadcast_to(edges_ref[...].T[None, :levels], edge_ref.shape)


HBM = pl.BlockSpec(memory_space=pltpu.HBM)
VMEM = pl.BlockSpec(memory_space=pltpu.VMEM)


def mixed_levels(ring, field, vertical, rate):
    levels, lats, lons = field.shape
    groups, rows = lats // SUB, levels * SUB
    return pl.pallas_call(
        functools.partial(mix_kernel, groups),
        in_specs=[HBM] * 3,
        out_specs=[VMEM] * 4,
        out_shape=[
            jax.ShapeDtypeStruct((groups, rows, lons), jnp.float32),
            jax.ShapeDtypeStruct((ring, levels, LANES), jnp.float32),
            jax.ShapeDtypeStruct((levels, LANES), jnp.float32),
            jax.ShapeDtypeStruct((2, LANES, LANES), jnp.float32),
        ],
        scratch_shapes=[
            pltpu.VMEM((groups, levels, SUB, lons), jnp.float32),
            pltpu.VMEM(vertical.shape, jnp.float32),
            pltpu.VMEM(rate.shape, jnp.float32),
            pltpu.VMEM((2, rows, rows), jnp.bfloat16),
            pltpu.VMEM((LANES, LANES), jnp.float32),
            pltpu.SemaphoreType.DMA((groups + 2,)),
        ],
        compiler_params=pltpu.CompilerParams(vmem_limit_bytes=16 << 20),
        cost_estimate=pl.CostEstimate(flops=8 * 10**8, bytes_accessed=5 * 10**6, transcendentals=2 * 10**5),
        name="mix",
    )(*[pltpu.with_memory_space_constraint(v, pltpu.HBM) for v in (field, vertical, rate)])


def filter_kernel(batch, place_ref, decay_ref, turned_ref, edge_ref, mixed_ref, out_ref, state_ref):
    groups, rows, lons = mixed_ref.shape
    ring, levels, _ = edge_ref.shape
    tiles = lons // LANES
    log_decay = decay_ref[...]
    eastward = iota((levels, LANES), 1) < MID
    total = jnp.zeros((levels, LANES), jnp.float32)
    for device in range(ring):
        away = (place_ref[0] + ring - device) % ring
        blocks = jnp.where(eastward, (away + ring - 1) % ring, ring - 1 - away).astype(jnp.float32)
        total = total + edge_ref[device] * jnp.exp(blocks * (lons * log_decay))
    total = total / (1.0 - jnp.exp((ring * lons) * log_decay))
    state_ref[...] = jnp.concatenate([total, jnp.zeros((LANES - levels, LANES), jnp.float32)], 0).T
    source, target = iota((2 * LANES, 2 * LANES), 0) % LANES, iota((2 * LANES, 2 * LANES), 1)
    sums_east = ((source <= target) | (target >= LANES)).astype(jnp.bfloat16)
    sums_west = ((source > target) | (target >= LANES)).astype(jnp.bfloat16)
    offset = (iota((rows, LANES), 1) - MID).astype(jnp.float32)
    for first_group in range(0, groups, batch):
        batched = range(first_group, first_group + batch)
        falling, rising, half, from_east, from_west = [], [], [], [], []
        for g in batched:
            here = slice(g * SUB, (g + 1) * SUB)
            log_decay, gain = columns(turned_ref[0, here], levels), columns(turned_ref[1, here], levels)
            falling.append(jnp.exp(offset * log_decay))
            rising.append(jnp.exp(-offset * log_decay))
            half.append(jnp.exp(MID * log_decay))
            for scale, pieces in ((rising[-1] * gain, from_east), (falling[-1] * gain, from_west)):
                pieces += [jnp.concatenate(split(mixed_ref[g, :, c * LANES : (c + 1) * LANES] * scale), 1) for c in range(tiles)]
        sums = [dot(jnp.concatenate(pieces, 0), table) for pieces, table in ((from_east, sums_east), (from_west, sums_west))]
        for at, g in enumerate(batched):
            east, west = ([s[(at * tiles + c) * rows : (at * tiles + c + 1) * rows] for c in range(tiles)] for s in sums)
            carry = half[at] * columns(state_ref[g * SUB : (g + 1) * SUB], levels)
            for c in range(tiles):
                onward = half[at] * (half[at] * (east[c][:, LANES:] + carry))
                east[c] = east[c][:, :LANES] + carry
                carry = onward
            carry = half[at] * columns(state_ref[MID + g * SUB : MID + (g + 1) * SUB], levels)
            for c in range(tiles - 1, -1, -1):
                onward = half[at] * (half[at] * (west[c][:, LANES:] + carry))
                west[c] = west[c][:, :LANES] + carry
                carry = onward
            for c in range(tiles):
                filtered = falling[at] * east[c] + rising[at] * west[c]
                out_ref[:, :, g * tiles + c] = filtered.reshape(levels // 2, 2, SUB, LANES)


def filtered_blocks(where, decay, turned, edges, mixed):
    groups, rows, lons = mixed.shape
    levels, tiles = rows // SUB, lons // LANES
    return pl.pallas_call(
        functools.partial(filter_kernel, groups),
        in_specs=[pl.BlockSpec(memory_space=pltpu.SMEM)] + [VMEM] * 4,
        out_specs=VMEM,
        out_shape=jax.ShapeDtypeStruct((levels // 2, 2, groups * tiles, SUB, LANES), jnp.float32),
        scratch_shapes=[pltpu.VMEM((LANES, LANES), jnp.float32)],
        compiler_params=pltpu.CompilerParams(vmem_limit_bytes=16 << 20),
        cost_estimate=pl.CostEstimate(flops=8 * 10**8, bytes_accessed=5 * 10**6, transcendentals=2 * 10**5),
        name="filter",
    )(where, decay, turned, edges, mixed)


def convolve_kernel(values_ref, kernel_ref, out_ref, high_ref, low_ref):
    sources, parts, lats, lons = out_ref.shape
    tiles = lons // LANES
    groups = lats // SUB
    strips = []
    for part in range(parts):
        for c in range(tiles):
            strips.append(jnp.concatenate([values_ref[source, part, g * tiles + c] for source in range(sources) for g in range(groups)], 0))
    f_high, f_low = split(jnp.concatenate(strips, 1))
    group = 4
    for j in range(0, sources, group):
        k_high, k_low = split(kernel_ref[j * lats : (j + group) * lats])
        result = dot3(k_high, k_low, f_high, f_low)
        for part in range(parts):
            out_ref[j : j + group, part] = result[:, part * lons : (part + 1) * lons].reshape(group, lats, lons)


def convolved(values, lat_kernel, lats, lons):
    sources = values.shape[0]
    nlat = sources * lats
    return pl.pallas_call(
        convolve_kernel,
        in_specs=[VMEM] * 2,
        out_specs=VMEM,
        out_shape=jax.ShapeDtypeStruct((sources, 2, lats, lons), jnp.float32),
        scratch_shapes=[
            pltpu.VMEM((nlat, 2 * lons), jnp.bfloat16),
            pltpu.VMEM((nlat, 2 * lons), jnp.bfloat16),
        ],
        compiler_params=pltpu.CompilerParams(vmem_limit_bytes=16 << 20),
        cost_estimate=pl.CostEstimate(flops=28 * 10**8, bytes_accessed=8 * 10**6, transcendentals=0),
        name="convolve",
    )(values, lat_kernel)


def on_device(field, vertical, rate, lat_kernel):
    ring = lax.axis_size("lon")
    levels, lats, lons = field.shape
    where = lax.axis_index("lon").reshape(1)

    def exchanged(v, axis):
        return lax.all_to_all(v, axis, 0, 0, tiled=True)

    mixed, edges, decay, turned = mixed_levels(ring, field, vertical, rate)
    where, edges = lax.optimization_barrier((where, edges))
    values = filtered_blocks(where, decay, turned, exchanged(edges, "lon"), mixed)
    out = convolved(exchanged(values, "lat"), lat_kernel, lats, lons)
    return exchanged(out, "lat").reshape(levels, lats, lons)


def solution(mesh):
    return jax.shard_map(
        on_device,
        mesh=mesh,
        in_specs=(P(None, "lat", "lon"), P(), P(None, "lat"), P()),
        out_specs=P(None, "lat", "lon"),
        check_vma=False,
    )
```

```python
import functools

import jax
import jax.numpy as jnp
from jax import lax
from jax.experimental import pallas as pl
from jax.experimental.pallas import tpu as pltpu
from jax.sharding import PartitionSpec as P

LANES = 128
SUB = 8
MID = LANES // 2


def split(x):
    high = x.astype(jnp.bfloat16)
    return high, (x - high.astype(jnp.float32)).astype(jnp.bfloat16)


def dot(a, b):
    return jnp.dot(a, b, preferred_element_type=jnp.float32)


def dot3(a_high, a_low, b_high, b_low):
    return dot(a_high, b_high) + (dot(a_high, b_low) + dot(a_low, b_high))


def iota(shape, dim):
    return lax.broadcasted_iota(jnp.int32, shape, dim)


def log_decays(rate):
    decay = 1.0 - rate
    gap = decay - 1.0
    return jnp.log(decay) * (rate / -gap)


def columns(tile, levels):
    return jnp.concatenate([jnp.broadcast_to(tile[:, k : k + 1], (SUB, LANES)) for k in range(levels)], 0)


def mix_kernel(batch, field_hbm, vertical_hbm, rate_hbm, mixed_ref, edge_ref, decay_ref, turned_ref, sums_ref, field_ref, vertical_ref, rate_ref, matrix_ref, edges_ref, sems):
    groups, rows, lons = mixed_ref.shape
    levels = rows // SUB
    lats = groups * SUB
    tiles = lons // LANES
    small = [
        pltpu.make_async_copy(rate_hbm, rate_ref, sems.at[groups]),
        pltpu.make_async_copy(vertical_hbm, vertical_ref, sems.at[groups + 1]),
    ]
    for copy in small:
        copy.start()
    copies = [pltpu.make_async_copy(field_hbm.at[:, pl.ds(g * SUB, SUB), :], field_ref.at[g], sems.at[g]) for g in range(groups)]
    for copy in copies:
        copy.start()
    spread = (iota((rows, levels), 0) // SUB == iota((rows, levels), 1)).astype(jnp.bfloat16)
    across = (iota((levels, rows), 1) // SUB == iota((levels, rows), 0)).astype(jnp.bfloat16)
    same = iota((rows, rows), 0) % SUB == iota((rows, rows), 1) % SUB
    ones = jnp.ones((2 * LANES, LANES), jnp.bfloat16)
    source, target = iota((2 * LANES, 2 * LANES), 0) % LANES, iota((2 * LANES, 2 * LANES), 1)
    sums_ref[0] = ((source <= target) | (target >= LANES)).astype(jnp.bfloat16)
    sums_ref[1] = ((source > target) | (target >= LANES)).astype(jnp.bfloat16)
    edges_ref[...] = jnp.zeros_like(edges_ref)
    small[0].wait()
    filled = jnp.full((levels, MID - lats), 0.5, jnp.float32)
    rate = rate_ref[...]
    rate = jnp.concatenate([rate, filled, rate, filled], 1)
    rest = jnp.zeros((LANES - levels, LANES), jnp.float32)
    log_decay = log_decays(rate)
    decay_ref[...] = log_decay
    turned_ref[0] = jnp.concatenate([log_decay, rest], 0).T
    turned_ref[1] = jnp.concatenate([rate / (2.0 - rate), rest], 0).T
    small[1].wait()
    for i, piece in enumerate(split(vertical_ref[...])):
        tall = dot(spread, piece).astype(jnp.bfloat16)
        matrix_ref[i] = jnp.where(same, dot(tall, across), 0.0).astype(jnp.bfloat16)

    lane = iota((rows, LANES), 1).astype(jnp.float32)
    narrow = iota((SUB, LANES), 1)
    weighted = []
    for first_group in range(0, groups, batch):
        batched = range(first_group, first_group + batch)
        for g in batched:
            copies[g].wait()
        x_high, x_low = split(jnp.concatenate([field_ref[g].reshape(rows, lons) for g in batched], 1))
        mixed_batch = dot3(matrix_ref[0], matrix_ref[1], x_high, x_low)
        for at, g in enumerate(batched):
            mixed = mixed_batch[:, at * lons : (at + 1) * lons]
            mixed_ref[g] = mixed
            value = [mixed[:, c * LANES : (c + 1) * LANES] for c in range(tiles)]
            here = slice(g * SUB, (g + 1) * SUB)
            log_decay = columns(turned_ref[0, here], levels)
            hop = jnp.exp(float(LANES) * log_decay)
            last, first = value[0], value[-1]
            for c in range(1, tiles):
                last = last * hop + value[c]
                first = first * hop + value[tiles - 1 - c]
            last = last * jnp.exp((LANES - lane) * log_decay)
            first = first * jnp.exp(lane * log_decay)
            weighted += [(last, g * SUB, here), (first, MID + g * SUB, here)]
    totals = dot(jnp.concatenate([jnp.concatenate(split(v), 1) for v, _, _ in weighted], 0), ones)
    for i, (_, base, here) in enumerate(weighted):
        edges = jnp.zeros((SUB, LANES), jnp.float32)
        for k in range(levels):
            at = i * rows + k * SUB
            edges = jnp.where(narrow == k, totals[at : at + SUB], edges)
        edges_ref[base : base + SUB, :] = edges * turned_ref[1, here]
    edge_ref[...] = jnp.broadcast_to(edges_ref[...].T[None, :levels], edge_ref.shape)


HBM = pl.BlockSpec(memory_space=pltpu.HBM)
VMEM = pl.BlockSpec(memory_space=pltpu.VMEM)


def mixed_levels(ring, field, vertical, rate):
    levels, lats, lons = field.shape
    groups, rows = lats // SUB, levels * SUB
    return pl.pallas_call(
        functools.partial(mix_kernel, groups),
        in_specs=[HBM] * 3,
        out_specs=[VMEM] * 5,
        out_shape=[
            jax.ShapeDtypeStruct((groups, rows, lons), jnp.float32),
            jax.ShapeDtypeStruct((ring, levels, LANES), jnp.float32),
            jax.ShapeDtypeStruct((levels, LANES), jnp.float32),
            jax.ShapeDtypeStruct((2, LANES, LANES), jnp.float32),
            jax.ShapeDtypeStruct((2, 2 * LANES, 2 * LANES), jnp.bfloat16),
        ],
        scratch_shapes=[
            pltpu.VMEM((groups, levels, SUB, lons), jnp.float32),
            pltpu.VMEM(vertical.shape, jnp.float32),
            pltpu.VMEM(rate.shape, jnp.float32),
            pltpu.VMEM((2, rows, rows), jnp.bfloat16),
            pltpu.VMEM((LANES, LANES), jnp.float32),
            pltpu.SemaphoreType.DMA((groups + 2,)),
        ],
        compiler_params=pltpu.CompilerParams(vmem_limit_bytes=16 << 20),
        cost_estimate=pl.CostEstimate(flops=8 * 10**8, bytes_accessed=5 * 10**6, transcendentals=2 * 10**5),
        name="mix",
    )(*[pltpu.with_memory_space_constraint(v, pltpu.HBM) for v in (field, vertical, rate)])


def filter_kernel(batch, place_ref, decay_ref, turned_ref, sums_ref, edge_ref, mixed_ref, out_ref, state_ref):
    groups, rows, lons = mixed_ref.shape
    ring, levels, _ = edge_ref.shape
    tiles = lons // LANES
    log_decay = decay_ref[...]
    eastward = iota((levels, LANES), 1) < MID
    total = jnp.zeros((levels, LANES), jnp.float32)
    for device in range(ring):
        away = (place_ref[0] + ring - device) % ring
        blocks = jnp.where(eastward, (away + ring - 1) % ring, ring - 1 - away).astype(jnp.float32)
        total = total + edge_ref[device] * jnp.exp(blocks * (lons * log_decay))
    total = total / (1.0 - jnp.exp((ring * lons) * log_decay))
    state_ref[...] = jnp.concatenate([total, jnp.zeros((LANES - levels, LANES), jnp.float32)], 0).T
    sums_east, sums_west = sums_ref[0], sums_ref[1]
    offset = (iota((rows, LANES), 1) - MID).astype(jnp.float32)
    for first_group in range(0, groups, batch):
        batched = range(first_group, first_group + batch)
        falling, rising, half, from_east, from_west = [], [], [], [], []
        for g in batched:
            here = slice(g * SUB, (g + 1) * SUB)
            log_decay, gain = columns(turned_ref[0, here], levels), columns(turned_ref[1, here], levels)
            falling.append(jnp.exp(offset * log_decay))
            rising.append(jnp.exp(-offset * log_decay))
            half.append(jnp.exp(MID * log_decay))
            for scale, pieces in ((rising[-1] * gain, from_east), (falling[-1] * gain, from_west)):
                pieces += [jnp.concatenate(split(mixed_ref[g, :, c * LANES : (c + 1) * LANES] * scale), 1) for c in range(tiles)]
        sums = [dot(jnp.concatenate(pieces, 0), table) for pieces, table in ((from_east, sums_east), (from_west, sums_west))]
        for at, g in enumerate(batched):
            east, west = ([s[(at * tiles + c) * rows : (at * tiles + c + 1) * rows] for c in range(tiles)] for s in sums)
            carry = half[at] * columns(state_ref[g * SUB : (g + 1) * SUB], levels)
            for c in range(tiles):
                onward = half[at] * (half[at] * (east[c][:, LANES:] + carry))
                east[c] = east[c][:, :LANES] + carry
                carry = onward
            carry = half[at] * columns(state_ref[MID + g * SUB : MID + (g + 1) * SUB], levels)
            for c in range(tiles - 1, -1, -1):
                onward = half[at] * (half[at] * (west[c][:, LANES:] + carry))
                west[c] = west[c][:, :LANES] + carry
                carry = onward
            for c in range(tiles):
                filtered = falling[at] * east[c] + rising[at] * west[c]
                out_ref[:, :, g * tiles + c] = filtered.reshape(levels // 2, 2, SUB, LANES)


def filtered_blocks(where, decay, turned, sums, edges, mixed):
    groups, rows, lons = mixed.shape
    levels, tiles = rows // SUB, lons // LANES
    return pl.pallas_call(
        functools.partial(filter_kernel, groups),
        in_specs=[pl.BlockSpec(memory_space=pltpu.SMEM)] + [VMEM] * 5,
        out_specs=VMEM,
        out_shape=jax.ShapeDtypeStruct((levels // 2, 2, groups * tiles, SUB, LANES), jnp.float32),
        scratch_shapes=[pltpu.VMEM((LANES, LANES), jnp.float32)],
        compiler_params=pltpu.CompilerParams(vmem_limit_bytes=16 << 20),
        cost_estimate=pl.CostEstimate(flops=8 * 10**8, bytes_accessed=5 * 10**6, transcendentals=2 * 10**5),
        name="filter",
    )(where, decay, turned, sums, edges, mixed)


def convolve_kernel(values_ref, kernel_ref, out_ref, high_ref, low_ref):
    sources, parts, lats, lons = out_ref.shape
    tiles = lons // LANES
    groups = lats // SUB
    strips = []
    for part in range(parts):
        for c in range(tiles):
            strips.append(jnp.concatenate([values_ref[source, part, g * tiles + c] for source in range(sources) for g in range(groups)], 0))
    f_high, f_low = split(jnp.concatenate(strips, 1))
    group = 4
    for j in range(0, sources, group):
        k_high, k_low = split(kernel_ref[j * lats : (j + group) * lats])
        result = dot3(k_high, k_low, f_high, f_low)
        for part in range(parts):
            out_ref[j : j + group, part] = result[:, part * lons : (part + 1) * lons].reshape(group, lats, lons)


def convolved(values, lat_kernel, lats, lons):
    sources = values.shape[0]
    nlat = sources * lats
    return pl.pallas_call(
        convolve_kernel,
        in_specs=[VMEM] * 2,
        out_specs=VMEM,
        out_shape=jax.ShapeDtypeStruct((sources, 2, lats, lons), jnp.float32),
        scratch_shapes=[
            pltpu.VMEM((nlat, 2 * lons), jnp.bfloat16),
            pltpu.VMEM((nlat, 2 * lons), jnp.bfloat16),
        ],
        compiler_params=pltpu.CompilerParams(vmem_limit_bytes=16 << 20),
        cost_estimate=pl.CostEstimate(flops=28 * 10**8, bytes_accessed=8 * 10**6, transcendentals=0),
        name="convolve",
    )(values, lat_kernel)


def on_device(field, vertical, rate, lat_kernel):
    ring = lax.axis_size("lon")
    levels, lats, lons = field.shape
    where = lax.axis_index("lon").reshape(1)

    def exchanged(v, axis):
        return lax.all_to_all(v, axis, 0, 0, tiled=True)

    mixed, edges, decay, turned, sums = mixed_levels(ring, field, vertical, rate)
    where, edges = lax.optimization_barrier((where, edges))
    values = filtered_blocks(where, decay, turned, sums, exchanged(edges, "lon"), mixed)
    out = convolved(exchanged(values, "lat"), lat_kernel, lats, lons)
    return exchanged(out, "lat").reshape(levels, lats, lons)


def solution(mesh):
    return jax.shard_map(
        on_device,
        mesh=mesh,
        in_specs=(P(None, "lat", "lon"), P(), P(None, "lat"), P()),
        out_specs=P(None, "lat", "lon"),
        check_vma=False,
    )
```
